32 devices in a mesh: gx: 8 (over y, x, core), gy: 4 (over z).
Axes of the slice: x: 2, y: 2, z: 4, core: 2. Of those that a mesh axis runs over, the one named last changes fastest.
Arguments:
- checkpoint: float32 [27, 32, 64, 128], P(None, 'gx', 'gy'), may hold values from 0.0001 to 0.5, as said below
- later_adjoint: float32 [27, 32, 64, 128], P(None, 'gx', 'gy'), may hold values from -6 to 6
- resistance: float32 [32, 64, 128], P('gx', 'gy'), may hold values from 0.05 to 0.8
- solid_mask: int32 [32, 64, 128], P('gx', 'gy'), may hold values from 0 to 1, as said below
Outputs:
- adjoint_start: float32 [27, 32, 64, 128], P(None, 'gx', 'gy')
- sensitivity: float32 [32, 64, 128], P('gx', 'gy')
The draws below stay inside these ranges and needn't reach their ends.
Inputs may be any that keep to these rules, and one draw needn't show every extreme that they name: `checkpoint`: positive populations near equilibrium, with mean x velocity rising along x. `solid_mask`: solid grains are balls inside aligned 8 x 8 x 8 bricks; every brick keeps fluid at its corners.
All inputs are finite; a program needn't handle non-finite values.
Results may differ from the reference program's by a relative error of at most 0.0003.
Values sent between devices are 32-bit elements; how exact they have to be, the bound alone decides.
A program may use at most 64 MiB of HBM per device.

```python
import math
import jax
import jax.numpy as jnp
import numpy as np
from jax import lax

NZ = 128
STEPS = 4
NX = 32
NY = 64


def draw_checkpoint(key, part):
    key_list = jax.random.split(jax.random.fold_in(key, 11), 6)
    shape_grid = (NX, NY, NZ)
    position_x = jnp.arange(NX).astype(jnp.float32)[:, None, None] / NX
    density = 1.0 + 0.03 * jnp.clip(jax.random.normal(key_list[0], shape_grid, jnp.float32), -1.5, 1.5)
    velocity_x = 0.04 * (1.0 + 2.0 * position_x) + 0.01 * jnp.clip(jax.random.normal(key_list[1], shape_grid, jnp.float32), -2.0, 2.0)
    amplitude = jnp.exp(jax.random.uniform(key_list[2], shape_grid, jnp.float32, math.log(0.01), math.log(0.1)))
    velocity_y = 0.02 * jax.random.uniform(key_list[3], shape_grid, jnp.float32, -1.0, 1.0)
    velocity_z = 0.02 * jax.random.uniform(key_list[4], shape_grid, jnp.float32, -1.0, 1.0)
    speed_list = [[first_comp, second_comp, third_comp] for first_comp in (-1, 0, 1) for second_comp in (-1, 0, 1) for third_comp in (-1, 0, 1)]
    weight_table = [8.0 / 27.0, 2.0 / 27.0, 1.0 / 54.0, 1.0 / 216.0]
    weight_list = [weight_table[entry[0] * entry[0] + entry[1] * entry[1] + entry[2] * entry[2]] for entry in speed_list]
    speed_x = jnp.asarray([entry[0] for entry in speed_list], jnp.float32).reshape(27, 1, 1, 1)
    speed_y = jnp.asarray([entry[1] for entry in speed_list], jnp.float32).reshape(27, 1, 1, 1)
    speed_z = jnp.asarray([entry[2] for entry in speed_list], jnp.float32).reshape(27, 1, 1, 1)
    projected = speed_x * velocity_x + speed_y * velocity_y + speed_z * velocity_z
    speed_square = velocity_x * velocity_x + velocity_y * velocity_y + velocity_z * velocity_z
    equilibrium = jnp.asarray(weight_list, jnp.float32).reshape(27, 1, 1, 1) * density * (1.0 + 3.0 * projected + 4.5 * projected * projected - 1.5 * speed_square)
    noise = jax.random.uniform(key_list[5], (27,) + shape_grid, jnp.float32, -1.0, 1.0)
    return (equilibrium * (1.0 + amplitude * noise)).astype(jnp.float32)


def draw_solid_mask(key, part):
    key_list = jax.random.split(jax.random.fold_in(key, 23), 3)
    brick_x = NX // 8
    brick_y = NY // 8
    brick_z = NZ // 8
    bricks = (brick_x, brick_y, brick_z)
    present = jax.random.randint(key_list[0], bricks, 0, 10) < 7
    first_brick = (jnp.arange(brick_x)[:, None, None] == 0) & (jnp.arange(brick_y)[None, :, None] == 0) & (jnp.arange(brick_z)[None, None, :] == 0)
    present = present | first_brick
    centre = jax.random.randint(key_list[1], bricks + (3,), 2, 6)
    radius = jax.random.randint(key_list[2], bricks, 2, 4)
    inside = jnp.arange(8)
    offset_x = inside.reshape(1, 8, 1, 1, 1, 1) - centre[..., 0].reshape(brick_x, 1, brick_y, 1, brick_z, 1)
    offset_y = inside.reshape(1, 1, 1, 8, 1, 1) - centre[..., 1].reshape(brick_x, 1, brick_y, 1, brick_z, 1)
    offset_z = inside.reshape(1, 1, 1, 1, 1, 8) - centre[..., 2].reshape(brick_x, 1, brick_y, 1, brick_z, 1)
    distance = offset_x * offset_x + offset_y * offset_y + offset_z * offset_z
    limit = (radius * radius).reshape(brick_x, 1, brick_y, 1, brick_z, 1)
    solid_cells = present.reshape(brick_x, 1, brick_y, 1, brick_z, 1) & (distance < limit)
    return solid_cells.astype(jnp.int32).reshape(NX, NY, NZ)


def shard_levels(rng, extent, cuts, smallest, high):
    level = 1.0
    for axis_at, blocks in cuts:
        steps = jax.random.uniform(jax.random.fold_in(jax.random.fold_in(rng, 6), axis_at), (blocks,), jnp.float32, smallest / len(cuts), high / len(cuts))
        level = level * jnp.repeat(jnp.exp(steps), extent[axis_at] // blocks).reshape((-1,) + (1,) * (len(extent) - 1 - axis_at))
    return level


def centred(rng, extent, width, bound, cuts=(), kind=jnp.bfloat16):
    drawn = width * jax.random.normal(rng, extent, jnp.float32)
    if cuts:
        drawn = drawn * shard_levels(rng, extent, cuts, -0.22, 0.18)
    return jnp.clip(drawn, -bound, bound).astype(kind)


def setup_inputs(seed: int = 0) -> dict:
    arg_keys = jax.random.split(jax.random.key(seed), 5)
    checkpoint = draw_checkpoint(jax.random.fold_in(arg_keys[4], 71), 0)
    later_adjoint = centred(arg_keys[1], (27, NX, NY, NZ), 1.0, 6.0, ((1, 8), (2, 4)), jnp.float32)
    resistance = jnp.clip(jnp.exp(math.log(0.8) - 2.7725887 * jax.random.uniform(arg_keys[2], (NX, NY, NZ), jnp.float32) ** shard_levels(arg_keys[2], (NX, NY, NZ), ((0, 8), (1, 4)), -0.2, 0.2)), 0.05, 0.8)
    solid_mask = draw_solid_mask(jax.random.fold_in(arg_keys[4], 71), 0)
    return dict(checkpoint=checkpoint, later_adjoint=later_adjoint, resistance=resistance, solid_mask=solid_mask)


relax_rate = 1.0 / 1.04
body_force = 0.0001
entropy_floor = 0.0002
seed_gain = 25.0

def lattice_tables():
    speed_list = [[first_comp, second_comp, third_comp] for first_comp in (-1, 0, 1) for second_comp in (-1, 0, 1) for third_comp in (-1, 0, 1)]
    weight_table = [8.0 / 27.0, 2.0 / 27.0, 1.0 / 54.0, 1.0 / 216.0]
    weight_list = [weight_table[entry[0] * entry[0] + entry[1] * entry[1] + entry[2] * entry[2]] for entry in speed_list]
    return (np.array(speed_list), np.array(weight_list))

def column(values_table, template):
    return jnp.asarray(values_table, dtype=template.dtype).reshape((-1,) + (1,) * (template.ndim - 1))

def collide(populations, resistance, solid_cells):
    speeds, weights = lattice_tables()
    weight_col = column(weights, populations)
    speed_cols = [column(speeds[:, axis_pos], populations) for axis_pos in range(3)]
    density = lax.optimization_barrier(jnp.sum(populations, axis=0))
    moments = [lax.optimization_barrier(jnp.sum(speed_cols[axis_pos] * populations, axis=0)) for axis_pos in range(3)]
    forces = [density * body_force - resistance * moments[0], -resistance * moments[1], -resistance * moments[2]]
    velocity = [(moments[axis_pos] + 0.5 * forces[axis_pos]) / density for axis_pos in range(3)]
    projected = speed_cols[0] * velocity[0] + speed_cols[1] * velocity[1] + speed_cols[2] * velocity[2]
    speed_square = velocity[0] * velocity[0] + velocity[1] * velocity[1] + velocity[2] * velocity[2]
    equilibrium = weight_col * density * (1.0 + 3.0 * projected + 4.5 * projected * projected - 1.5 * speed_square)
    departure = populations - equilibrium
    shear_part = jnp.zeros_like(populations)
    for first_axis in range(3):
        for second_axis in range(first_axis, 3):
            product = speeds[:, first_axis] * speeds[:, second_axis]
            stress = lax.optimization_barrier(jnp.sum(column(product, populations) * departure, axis=0))
            if first_axis == second_axis:
                hermite = product - 1.0 / 3.0
            else:
                hermite = 2.0 * product
            shear_part = shear_part + column(hermite, populations) * stress
    shear_part = 4.5 * weight_col * shear_part
    higher = departure - shear_part
    inverse_weight = column(1.0 / weights, populations)
    shear_shear = lax.optimization_barrier(jnp.sum(shear_part * shear_part * inverse_weight, axis=0))
    shear_higher = lax.optimization_barrier(jnp.sum(shear_part * higher * inverse_weight, axis=0))
    higher_higher = lax.optimization_barrier(jnp.sum(higher * higher * inverse_weight, axis=0))
    stabilizer = 1.0 / relax_rate - (2.0 - 1.0 / relax_rate) * shear_higher / jnp.maximum(shear_shear + higher_higher, entropy_floor)
    force_along = speed_cols[0] * forces[0] + speed_cols[1] * forces[1] + speed_cols[2] * forces[2]
    force_velocity = forces[0] * velocity[0] + forces[1] * velocity[1] + forces[2] * velocity[2]
    source = weight_col * (3.0 * (force_along - force_velocity) + 9.0 * projected * force_along)
    relaxed = populations - relax_rate * (2.0 * shear_part + stabilizer * higher) + (1.0 - relax_rate) * source
    return jnp.where(solid_cells, populations[::-1], relaxed)

def propagate_whole(populations, direction):
    speeds, weights = lattice_tables()
    moved_list = []
    for position in range(27):
        offsets = tuple((int(direction * speeds[position, axis_pos]) for axis_pos in range(3)))
        moved_list.append(jnp.roll(populations[position], offsets, axis=(0, 1, 2)))
    return jnp.stack(moved_list)

def collide_planes(populations, resistance, solid_cells):

    def one_plane(items):
        return collide(items[0], items[1], items[2])
    result = lax.map(one_plane, (jnp.moveaxis(populations, 1, 0), resistance, solid_cells))
    return jnp.moveaxis(result, 0, 1)

def adjoint_planes(populations, resistance, solid_cells, cotangent):

    def one_plane(items):

        def local_map(state_in, resist_in):
            return collide(state_in, resist_in, items[2])
        outcome, pullback = jax.vjp(local_map, items[0], items[1])
        return pullback(items[3])
    back_state, back_resist = lax.map(one_plane, (jnp.moveaxis(populations, 1, 0), resistance, solid_cells, jnp.moveaxis(cotangent, 1, 0)))
    return (jnp.moveaxis(back_state, 0, 1), back_resist)

def reference(checkpoint, later_adjoint, resistance, solid_mask):
    speeds, weights = lattice_tables()
    solid_cells = solid_mask == 1
    fluid_share = (1 - solid_mask).astype(checkpoint.dtype)
    states = [checkpoint]
    current = checkpoint
    for step_number in range(STEPS):
        current = propagate_whole(collide_planes(current, resistance, solid_cells), 1)
        states.append(current)
    speed_x = column(speeds[:, 0], current)
    flux_x = lax.optimization_barrier(jnp.sum(speed_x * current, axis=0))
    flux_mean = jnp.sum(fluid_share * flux_x) / (NX * NY * NZ)
    adjoint = later_adjoint + seed_gain * flux_mean * speed_x * fluid_share
    sensitivity = jnp.zeros_like(resistance)
    for step_number in reversed(range(STEPS)):
        pulled = propagate_whole(adjoint, -1)
        adjoint, extra_term = adjoint_planes(states[step_number], resistance, solid_cells, pulled)
        sensitivity = sensitivity + extra_term
    return (adjoint, sensitivity)
```

```python
import functools

import jax
import jax.numpy as jnp
import numpy as np
from jax import lax
from jax.experimental import pallas as pl
from jax.experimental.pallas import tpu as pltpu
from jax.sharding import PartitionSpec as P

MESH = pl.DeviceIdType.MESH
STEPS = 4
BETA = 1.0 / 1.04
KAPPA = 2.0 - 1.0 / BETA
BODY_FORCE = 0.0001
FLOOR = 2e-4
GAIN = 25.0
SPEEDS = [(a, b, c) for a in (-1, 0, 1) for b in (-1, 0, 1) for c in (-1, 0, 1)]
WTABLE = (8.0 / 27.0, 2.0 / 27.0, 1.0 / 54.0, 1.0 / 216.0)
CLASS = [a * a + b * b + c * c for a, b, c in SPEEDS]
PAIRS = list(range(14, 27))
PW = [WTABLE[CLASS[i]] for i in PAIRS]
W0 = WTABLE[0]
DIRS = [(1, 0), (-1, 0), (0, 1), (0, -1), (1, 1), (1, -1), (-1, 1), (-1, -1)]
TILE = 8


def moving(dx, dy, sign):
    return [
        i
        for i, (a, b, c) in enumerate(SPEEDS)
        if (dx == 0 or a == sign * dx) and (dy == 0 or b == sign * dy)
    ]


def quad(xx, yy, zz, xy, xz, yz):
    xpy, xpz, ypz = xx + yy, xx + zz, yy + zz
    tot = xpy + zz
    s1, s2 = tot + xy, tot - xy
    a, b = xz + yz, xz - yz
    return [
        zz, ypz - yz, yy, ypz + yz,
        s2 - b, xpy - xy, s2 + b,
        xpz - xz, xx, xpz + xz,
        s1 - a, xpy + xy, s1 + a,
    ]


def linear(x, y, z):
    xmy, xpy = x - y, x + y
    return [z, y - z, y, y + z, xmy - z, xmy, xmy + z, x - z, x, x + z, xpy - z, xpy, xpy + z]


def even_moments(e):
    e14, e15, e16, e17, e18, e19, e20, e21, e22, e23, e24, e25, e26 = e
    a, b, n, c = e18 + e20, e24 + e26, e21 + e23, e15 + e17
    m, p, cy = a + e19, b + e25, c + e16
    mp = m + p
    xx = mp + (n + e22)
    yy = cy + mp
    zz = (e14 + c) + (a + b) + n
    d18, d24, d21, d15 = e20 - e18, e26 - e24, e23 - e21, e17 - e15
    total = xx + cy + e14
    return total, xx, yy, zz, p - m, d18 + d24 + d21, d15 + d24 - d18


def odd_moments(o):
    o14, o15, o16, o17, o18, o19, o20, o21, o22, o23, o24, o25, o26 = o
    m, p = o18 + o19 + o20, o24 + o25 + o26
    x = m + p + (o21 + o22 + o23)
    y = (o15 + o16 + o17) + p - m
    z = o14 + (o17 - o15) + (o20 - o18) + (o26 - o24) + (o23 - o21)
    return x, y, z


def by_class(values):
    sums = {}
    for i, v in zip(PAIRS, values):
        sums[CLASS[i]] = v if CLASS[i] not in sums else sums[CLASS[i]] + v
    return sums


def split(f):
    even = [f[i] + f[26 - i] for i in PAIRS]
    odd = [f[i] - f[26 - i] for i in PAIRS]
    return even, odd, f[13]


def prepare(even, odd, f0, resist):
    total, xx, yy, zz, xy, xz, yz = even_moments(even)
    rho = total + f0
    j = odd_moments(odd)
    force = [rho * BODY_FORCE - resist * j[0], -resist * j[1], -resist * j[2]]
    inv = 1.0 / rho
    v = [j[a] + 0.5 * force[a] for a in range(3)]
    u = [v[a] * inv for a in range(3)]
    uv = [u[0] * v[0], u[1] * v[1], u[2] * v[2], u[0] * v[1], u[0] * v[2], u[1] * v[2]]
    third = rho * (1.0 / 3.0)
    pi = [xx - third, yy - third, zz - third, xy, xz, yz]
    stress = [pi[k] - uv[k] for k in range(6)]
    trace = stress[0] + stress[1] + stress[2]
    base = rho - 1.5 * (uv[0] + uv[1] + uv[2])
    q0 = trace * (-1.0 / 3.0)
    q = quad(
        stress[0] + q0, stress[1] + q0, stress[2] + q0, 2.0 * stress[3], 2.0 * stress[4], 2.0 * stress[5]
    )
    q = [val + (1 - CLASS[i]) * q0 if CLASS[i] != 1 else val for i, val in zip(PAIRS, q)]
    low = base - 1.5 * trace
    t2 = quad(*[4.5 * pi[k] for k in range(3)], *[9.0 * pi[k] for k in range(3, 6)])
    cv = linear(*v)
    he = [even[n] - (2.0 * PW[n]) * (low + t2[n]) for n in range(13)]
    ho = [odd[n] - (6.0 * PW[n]) * cv[n] for n in range(13)]
    h0 = f0 - W0 * low
    qq = by_class([val * val for val in q])
    ss = 40.5 * (WTABLE[1] * qq[1] + WTABLE[2] * qq[2] + WTABLE[3] * qq[3]) + (20.25 * W0) * (q0 * q0)
    sh = q0 * h0
    for n in range(13):
        sh = sh + q[n] * he[n]
    sh = 4.5 * sh
    hs = by_class([he[n] * he[n] + ho[n] * ho[n] for n in range(13)])
    hh = (
        (0.5 / WTABLE[1]) * hs[1] + (0.5 / WTABLE[2]) * hs[2] + (0.5 / WTABLE[3]) * hs[3]
        + (1.0 / W0) * (h0 * h0)
    )
    size = ss + hh
    inv_size = 1.0 / jnp.maximum(size, FLOOR)
    ratio = sh * inv_size
    gamma = 1.0 / BETA - KAPPA * ratio
    return dict(
        even=even, odd=odd, f0=f0, resist=resist, rho=rho, j=j, force=force, inv=inv, v=v, u=u, uv=uv,
        stress=stress, trace=trace, base=base, q=q, q0=q0, he=he, ho=ho, h0=h0, size=size,
        inv_size=inv_size, ratio=ratio, gamma=gamma,
    )


def relax(s):
    bg = BETA * s["gamma"]
    keep = 1.0 - bg
    kap = bg - 2.0 * BETA
    u, v, force = s["u"], s["v"], s["force"]
    uf = u[0] * force[0] + u[1] * force[1] + u[2] * force[2]
    const = bg * s["base"] - 1.5 * kap * s["trace"] - (3.0 * (1.0 - BETA)) * uf
    src = 9.0 * (1.0 - BETA)
    b45, k45, b9, k9 = 4.5 * bg, 4.5 * kap, 9.0 * bg, 9.0 * kap
    uv, st = s["uv"], s["stress"]
    t = [b45 * uv[a] + k45 * st[a] + src * (u[a] * force[a]) for a in range(3)]
    for n, (a, b) in enumerate(((0, 1), (0, 2), (1, 2))):
        t.append(b9 * uv[3 + n] + k9 * st[3 + n] + src * (u[a] * force[b] + u[b] * force[a]))
    tq = quad(*t)
    ck = linear(*[bg * v[a] + (1.0 - BETA) * force[a] for a in range(3)])
    even = [keep * s["even"][n] + (2.0 * PW[n]) * (const + tq[n]) for n in range(13)]
    odd = [keep * s["odd"][n] + (6.0 * PW[n]) * ck[n] for n in range(13)]
    return even, odd, keep * s["f0"] + W0 * const


def pull(s, me, mo, m0):
    bg = BETA * s["gamma"]
    keep = 1.0 - bg
    kap = bg - 2.0 * BETA
    u, v, force, uv, st = s["u"], s["v"], s["force"], s["uv"], s["stress"]
    q, q0, he, ho, h0 = s["q"], s["q0"], s["he"], s["ho"], s["h0"]
    off = ((0, 1), (0, 2), (1, 2))

    keep_bar = m0 * s["f0"]
    for n in range(13):
        keep_bar = keep_bar + (me[n] * s["even"][n] + mo[n] * s["odd"][n])
    mom = even_moments([(2.0 * PW[n]) * me[n] for n in range(13)])
    const_bar = mom[0] + W0 * m0
    tb = mom[1:]
    kb = odd_moments([(6.0 * PW[n]) * mo[n] for n in range(13)])
    bg_bar = (
        const_bar * s["base"]
        + 4.5 * (tb[0] * uv[0] + tb[1] * uv[1] + tb[2] * uv[2])
        + 9.0 * (tb[3] * uv[3] + tb[4] * uv[4] + tb[5] * uv[5])
        + (kb[0] * v[0] + kb[1] * v[1] + kb[2] * v[2])
    )
    kap_bar = (
        -1.5 * s["trace"] * const_bar
        + 4.5 * (tb[0] * st[0] + tb[1] * st[1] + tb[2] * st[2])
        + 9.0 * (tb[3] * st[3] + tb[4] * st[4] + tb[5] * st[5])
    )
    gamma_bar = BETA * (bg_bar + kap_bar - keep_bar)
    base_bar = bg * const_bar
    uf_bar = (-3.0 * (1.0 - BETA)) * const_bar

    scaled = KAPPA * gamma_bar * s["inv_size"]
    sh_bar = -4.5 * scaled
    size_bar = jnp.where(s["size"] > FLOOR, scaled * s["ratio"], 0.0)
    by_w = {k: size_bar * (1.0 / WTABLE[k]) for k in (1, 2, 3)}
    heb = [by_w[CLASS[i]] * he[n] + sh_bar * q[n] for n, i in enumerate(PAIRS)]
    hob = [by_w[CLASS[i]] * ho[n] for n, i in enumerate(PAIRS)]
    h0b = (size_bar * (2.0 / W0)) * h0 + sh_bar * q0
    by_q = {k: size_bar * (81.0 * WTABLE[k]) for k in (1, 2, 3)}
    qb = [sh_bar * he[n] + by_q[CLASS[i]] * q[n] for n, i in enumerate(PAIRS)]
    q0b = sh_bar * h0 + (size_bar * (40.5 * W0)) * q0

    hm = even_moments([(2.0 * PW[n]) * heb[n] for n in range(13)])
    low_bar = -(hm[0] + W0 * h0b)
    t2 = [-x for x in hm[1:]]
    hv = odd_moments([(6.0 * PW[n]) * hob[n] for n in range(13)])
    qm = even_moments(qb)
    q_all = (qm[0] + q0b) * (1.0 / 3.0)
    base_bar = base_bar + low_bar
    k45, k9 = 4.5 * kap, 9.0 * kap
    common = -1.5 * (kap * const_bar + low_bar) - q_all
    pb = [k45 * tb[a] + 4.5 * t2[a] + qm[1 + a] + common for a in range(3)]
    pb += [k9 * tb[a] + 9.0 * t2[a] + 2.0 * qm[1 + a] for a in range(3, 6)]

    that = [9.0 * tb[k] for k in range(6)]
    qhat = [bg * that[k] + 9.0 * t2[k] - (2.0 if k < 3 else 1.0) * pb[k] for k in range(6)]

    def apply(m, x):
        return [
            m[0] * x[0] + m[3] * x[1] + m[4] * x[2],
            m[3] * x[0] + m[1] * x[1] + m[5] * x[2],
            m[4] * x[0] + m[5] * x[1] + m[2] * x[2],
        ]

    qu = apply(qhat, u)
    tf = apply(that, force)
    tu = apply(that, u)
    rest = [((1.0 - BETA) * tf[a] + uf_bar * force[a]) * s["inv"] for a in range(3)]
    usq = u[0] * u[0] + u[1] * u[1] + u[2] * u[2]
    rho_bar = (
        base_bar * (1.0 + 1.5 * usq)
        - (pb[0] + pb[1] + pb[2]) * (1.0 / 3.0)
        - 0.5 * (u[0] * qu[0] + u[1] * qu[1] + u[2] * qu[2])
        - (u[0] * rest[0] + u[1] * rest[1] + u[2] * rest[2])
    )
    b3 = 3.0 * base_bar
    vb = [bg * kb[a] - hv[a] + qu[a] - b3 * u[a] + rest[a] for a in range(3)]
    fb = [(1.0 - BETA) * (kb[a] + tu[a]) + uf_bar * u[a] + 0.5 * vb[a] for a in range(3)]
    rho_bar = rho_bar + BODY_FORCE * fb[0]
    jb = [vb[a] - s["resist"] * fb[a] for a in range(3)]
    resist_bar = -(s["j"][0] * fb[0] + s["j"][1] * fb[1] + s["j"][2] * fb[2])
    pq = quad(*pb)
    jl = linear(*jb)
    eb = [keep * me[n] + heb[n] + rho_bar + pq[n] for n in range(13)]
    ob = [keep * mo[n] + hob[n] + jl[n] for n in range(13)]
    return eb, ob, keep * m0 + h0b + rho_bar, resist_bar


def kernel(
    nx, ny, cp_ref, la_ref, res_ref, mask_ref, out_ref, sens_ref,
    g, st, aux, fl, acc, ys, yr, cs, cr, ys0, yr0, cs0, cr0, sums, aux_sens,
    send, recv, send0, recv0, sum_send, sum_recv, la_sem,
):
    ext_x, ext_y, lanes = res_ref.shape
    tiles = ext_y // TILE
    chunks = ext_x * tiles
    top, end = TILE, TILE + ext_y
    px, py = lax.axis_index("gx"), lax.axis_index("gy")

    def device(dx, dy):
        return (lax.rem(px + (dx + nx), nx), lax.rem(py + (dy + ny), ny))

    partners = set((dx % nx, dy % ny) for dx, dy in DIRS)
    partners |= set((0, d) for d in range(1, ny)) | set((d, 0) for d in range(1, nx))
    partners = sorted(partners)
    barrier = pltpu.get_barrier_semaphore()
    for dx, dy in partners:
        pl.semaphore_signal(barrier, inc=1, device_id=device(dx, dy), device_id_type=MESH)

    la_copy = pltpu.make_async_copy(
        la_ref, g.at[2, :, pl.ds(1, ext_x), pl.ds(top, ext_y), :], la_sem
    )
    la_copy.start()
    fl[pl.ds(1, ext_x), pl.ds(top, ext_y), :] = 1.0 - mask_ref[...].astype(jnp.float32)

    def exchange(par, sign, first=False):
        ss, rs = (send0, recv0) if first else (send.at[par % 2], recv.at[par % 2])
        ysr, yrr = (ys0, yr0) if first else (ys.at[par % 2], yr.at[par % 2])
        csr, crr = (cs0, cr0) if first else (cs.at[par % 2], cr.at[par % 2])
        copies = []
        for d, (dx, dy) in enumerate(DIRS):
            if dy == 0:
                pops = moving(dx, 0, sign)
                lo = pops[0]
                near, far = (ext_x, 0) if dx > 0 else (1, ext_x + 1)
                rows = pl.ds(top, ext_y)
                src = g.at[par, pl.ds(lo, 9), near, rows, :]
                dst = g.at[par, pl.ds(lo, 9), far, rows, :]
            elif dx == 0:
                src, dst = ysr.at[d - 2], yrr.at[d - 2]
            else:
                src, dst = csr.at[d - 4], crr.at[d - 4]
            copies.append(
                pltpu.make_async_remote_copy(
                    src_ref=src, dst_ref=dst, send_sem=ss.at[d], recv_sem=rs.at[d],
                    device_id=device(dx, dy), device_id_type=MESH,
                )
            )
        if first:
            for d, (dx, dy) in enumerate(DIRS[:2]):
                near, far = (ext_x, 0) if dx > 0 else (1, ext_x + 1)
                rows = pl.ds(top, ext_y)
                copies.append(
                    pltpu.make_async_remote_copy(
                        src_ref=fl.at[near, rows, :], dst_ref=fl.at[far, rows, :],
                        send_sem=ss.at[8 + d], recv_sem=rs.at[8 + d],
                        device_id=device(dx, 0), device_id_type=MESH,
                    )
                )

        def pack_rows(unpack):
            for d, (dx, dy) in enumerate(DIRS):
                if dy == 0:
                    continue
                pops = moving(dx, dy, sign)
                if unpack:
                    row = top - 1 if dy > 0 else end
                    planes = [0 if dx > 0 else ext_x + 1] if dx else range(1, ext_x + 1)
                else:
                    row = end - 1 if dy > 0 else top
                    planes = [ext_x if dx > 0 else 1] if dx else range(1, ext_x + 1)
                box = (yrr if unpack else ysr) if dx == 0 else (crr if unpack else csr)
                k = d - 2 if dx == 0 else d - 4
                n = 0
                for i in pops:
                    for x in planes:
                        if unpack:
                            g[par, i, x, pl.ds(row, 1), :] = box[k, pl.ds(n, 1), :]
                        else:
                            box[k, pl.ds(n, 1), :] = g[par, i, x, pl.ds(row, 1), :]
                        n += 1
                if first:
                    for x in planes:
                        if unpack:
                            fl[x, pl.ds(row, 1), :] = box[k, pl.ds(n, 1), :]
                        else:
                            box[k, pl.ds(n, 1), :] = fl[x, pl.ds(row, 1), :]
                        n += 1

        def start():
            pack_rows(False)
            for copy in copies:
                copy.start()

        def finish():
            for copy in copies:
                copy.wait_recv()
            for copy in copies:
                copy.wait_send()
            pack_rows(True)

        return start, finish

    def place(c):
        x, t = c // tiles, lax.rem(c, tiles)
        return x, pl.multiple_of(t * TILE, TILE)

    def rolled(value, shift):
        return pltpu.roll(value, shift % lanes, 1) if shift else value

    def gather(par, x, row, sign):
        return [
            rolled(g[par, i, x + (1 - sign * a), pl.ds(row + (top - sign * b), TILE), :], sign * c)
            for i, (a, b, c) in enumerate(SPEEDS)
        ]

    def fluid_at(x, row, i):
        a, b, c = SPEEDS[i]
        return rolled(fl[x + (1 + a), pl.ds(row + (top + b), TILE), :], -c)

    def collided(f, x, row):
        solid = mask_ref[x, pl.ds(row, TILE), :] == 1
        even, odd, f0 = split(f)
        ne, no, n0 = relax(prepare(even, odd, f0, res_ref[x, pl.ds(row, TILE), :]))
        ne = [jnp.where(solid, even[n], ne[n]) * 0.5 for n in range(13)]
        no = [jnp.where(solid, -odd[n], no[n]) * 0.5 for n in range(13)]
        return ne, no, jnp.where(solid, f0, n0)

    def store_pairs(write, even, odd, f0):
        for n, i in enumerate(PAIRS):
            write(i, even[n] + odd[n])
            write(26 - i, even[n] - odd[n])
        write(13, f0)

    def into(par, x, row):
        def write(i, value):
            g[par, i, x + 1, pl.ds(row + top, TILE), :] = value
        return write

    def first_step(c, carry):
        x, row = place(c)
        f = [cp_ref[i, x, pl.ds(row, TILE), :] for i in range(27)]
        store_pairs(into(0, x, row), *collided(f, x, row))
        return carry

    lax.fori_loop(0, chunks, first_step, 0)
    start0, finish0 = exchange(0, 1)
    pl.semaphore_wait(barrier, len(partners))
    start0()
    la_copy.wait()
    start_la, finish_la = exchange(2, -1, first=True)
    start_la()
    finish0()
    for step in (1, 2):
        def forward_step(c, carry, step=step):
            x, row = place(c)
            f = gather((step - 1) % 2, x, row, 1)
            for i in range(27):
                st[step - 1, i, x, pl.ds(row, TILE), :] = f[i]
            store_pairs(into(step % 2, x, row), *collided(f, x, row))
            return carry

        lax.fori_loop(0, chunks, forward_step, 0)
        start, finish = exchange(step % 2, 1)
        start()
        if step == 1:
            finish_la()
        finish()

    def last_step(c, carry):
        x, row = place(c)
        f = gather(0, x, row, 1)
        for i in range(27):
            st[2, i, x, pl.ds(row, TILE), :] = f[i]
        ne, no, n0 = collided(f, x, row)
        for n, i in enumerate(PAIRS):
            if SPEEDS[i][0]:
                carry = carry + (
                    (ne[n] + no[n]) * fluid_at(x, row, i) - (ne[n] - no[n]) * fluid_at(x, row, 26 - i)
                )
        return carry

    part = lax.fori_loop(0, chunks, last_step, jnp.zeros((TILE, lanes), jnp.float32))

    def spread(slot, base, count, axis):
        copies = []
        for d in range(1, count):
            copies.append(
                pltpu.make_async_remote_copy(
                    src_ref=acc.at[slot], dst_ref=sums.at[base + d - 1],
                    send_sem=sum_send.at[base + d - 1], recv_sem=sum_recv.at[base + d - 1],
                    device_id=device(d, 0) if axis == 0 else device(0, d), device_id_type=MESH,
                )
            )
        return copies

    along_y, along_x = spread(0, 0, ny, 1), spread(1, ny - 1, nx, 0)
    acc[0] = part
    for copy in along_y:
        copy.start()

    def write_back(write, me, mo, m0, eb, ob, b0, solid):
        eb = [jnp.where(solid, me[n], eb[n]) for n in range(13)]
        ob = [jnp.where(solid, -mo[n], ob[n]) for n in range(13)]
        store_pairs(write, eb, ob, jnp.where(solid, m0, b0))

    def halves(m):
        even, odd, m0 = split(m)
        return [0.5 * e for e in even], [0.5 * o for o in odd], m0

    def adjoint_first(c, carry):
        x, row = place(c)
        rows = pl.ds(row, TILE)
        solid = mask_ref[x, rows, :] == 1
        f = [st[2, i, x, rows, :] for i in range(27)]
        s = prepare(*split(f), res_ref[x, rows, :])
        me, mo, m0 = halves(gather(2, x, row, -1))
        eb, ob, b0, rb = pull(s, me, mo, m0)
        write_back(into(1, x, row), me, mo, m0, eb, ob, b0, solid)
        sens_ref[x, rows, :] = jnp.where(solid, 0.0, rb)
        zero = jnp.zeros((TILE, lanes), jnp.float32)
        me, mo = [zero] * 13, [zero] * 13
        for n, i in enumerate(PAIRS):
            if SPEEDS[i][0]:
                ahead, behind = fluid_at(x, row, i), fluid_at(x, row, 26 - i)
                me[n], mo[n] = (0.5 * GAIN) * (ahead - behind), (0.5 * GAIN) * (ahead + behind)
        eb, ob, b0, rb = pull(s, me, mo, zero)

        def write(i, value):
            aux[i, x, rows, :] = value

        write_back(write, me, mo, zero, eb, ob, b0, solid)
        aux_sens[x, rows, :] = jnp.where(solid, 0.0, rb)
        return carry

    half = chunks // 2
    lax.fori_loop(0, half, adjoint_first, 0)
    for copy in along_y:
        copy.wait()
    total = acc[0]
    for d in range(ny - 1):
        total = total + sums[d]
    acc[1] = total
    for copy in along_x:
        copy.start()
    lax.fori_loop(half, chunks, adjoint_first, 0)
    for copy in along_x:
        copy.wait()
    for d in range(ny - 1, ny + nx - 2):
        total = total + sums[d]
    nodes = ext_x * ext_y * lanes * nx * ny
    mean = jnp.broadcast_to(jnp.sum(total, keepdims=True) * (1.0 / nodes), (TILE, lanes))

    def combine(c, carry):
        x, row = place(c)
        rows = pl.ds(row, TILE)
        inner = pl.ds(row + top, TILE)
        for i in range(27):
            g[1, i, x + 1, inner, :] = g[1, i, x + 1, inner, :] + mean * aux[i, x, rows, :]
        sens_ref[x, rows, :] = sens_ref[x, rows, :] + mean * aux_sens[x, rows, :]
        return carry

    lax.fori_loop(0, chunks, combine, 0)

    for step in (2, 1, 0):
        par = (step + 1) % 2
        start, finish = exchange(par, -1)
        start()
        finish()

        def adjoint_step(c, carry, step=step, par=par):
            x, row = place(c)
            rows = pl.ds(row, TILE)
            solid = mask_ref[x, rows, :] == 1
            if step:
                f = [st[step - 1, i, x, rows, :] for i in range(27)]
            else:
                f = [cp_ref[i, x, rows, :] for i in range(27)]
            s = prepare(*split(f), res_ref[x, rows, :])
            me, mo, m0 = halves(gather(par, x, row, -1))
            eb, ob, b0, rb = pull(s, me, mo, m0)

            def write(i, value):
                if step:
                    g[step % 2, i, x + 1, pl.ds(row + top, TILE), :] = value
                else:
                    out_ref[i, x, rows, :] = value

            write_back(write, me, mo, m0, eb, ob, b0, solid)
            sens_ref[x, rows, :] = sens_ref[x, rows, :] + jnp.where(solid, 0.0, rb)
            return carry

        lax.fori_loop(0, chunks, adjoint_step, 0)


def solution(mesh):
    nx, ny = mesh.shape["gx"], mesh.shape["gy"]

    def shards(checkpoint, later_adjoint, resistance, solid_mask):
        ext_x, ext_y, lanes = resistance.shape
        f32 = jnp.float32
        rows_x = 9 * ext_x
        vmem = pl.BlockSpec(memory_space=pltpu.VMEM)
        padded = (ext_x + 2, ext_y + 2 * TILE, lanes)
        count = nx + ny - 2
        return pl.pallas_call(
            functools.partial(kernel, nx, ny),
            out_shape=(
                jax.ShapeDtypeStruct(checkpoint.shape, f32),
                jax.ShapeDtypeStruct(resistance.shape, f32),
            ),
            in_specs=[vmem, pl.BlockSpec(memory_space=pl.ANY), vmem, vmem],
            out_specs=(vmem, vmem),
            scratch_shapes=[
                pltpu.VMEM((3, 27) + padded, f32),
                pltpu.VMEM((3, 27, ext_x, ext_y, lanes), f32),
                pltpu.VMEM((27, ext_x, ext_y, lanes), f32),
                pltpu.VMEM(padded, f32),
                pltpu.VMEM((2, TILE, lanes), f32),
                pltpu.VMEM((2, 2, rows_x, lanes), f32),
                pltpu.VMEM((2, 2, rows_x, lanes), f32),
                pltpu.VMEM((2, 4, 3, lanes), f32),
                pltpu.VMEM((2, 4, 3, lanes), f32),
                pltpu.VMEM((2, rows_x + ext_x, lanes), f32),
                pltpu.VMEM((2, rows_x + ext_x, lanes), f32),
                pltpu.VMEM((4, 4, lanes), f32),
                pltpu.VMEM((4, 4, lanes), f32),
                pltpu.VMEM((count, TILE, lanes), f32),
                pltpu.VMEM((ext_x, ext_y, lanes), f32),
                pltpu.SemaphoreType.DMA((2, 8)),
                pltpu.SemaphoreType.DMA((2, 8)),
                pltpu.SemaphoreType.DMA((10,)),
                pltpu.SemaphoreType.DMA((10,)),
                pltpu.SemaphoreType.DMA((count,)),
                pltpu.SemaphoreType.DMA((count,)),
                pltpu.SemaphoreType.DMA,
            ],
            compiler_params=pltpu.CompilerParams(
                collective_id=0, has_side_effects=True, vmem_limit_bytes=48 * 1024 * 1024
            ),
        )(checkpoint, later_adjoint, resistance, solid_mask)

    placed = (
        P(None, "gx", "gy", None),
        P(None, "gx", "gy", None),
        P("gx", "gy", None),
        P("gx", "gy", None),
    )
    return jax.shard_map(
        shards,
        mesh=mesh,
        in_specs=placed,
        out_specs=(P(None, "gx", "gy", None), P("gx", "gy", None)),
        check_vma=False,
    )
```

```python
import functools

import jax
import jax.numpy as jnp
import numpy as np
from jax import lax
from jax.experimental import pallas as pl
from jax.experimental.pallas import tpu as pltpu
from jax.sharding import PartitionSpec as P

MESH = pl.DeviceIdType.MESH
STEPS = 4
BETA = 1.0 / 1.04
KAPPA = 2.0 - 1.0 / BETA
BODY_FORCE = 0.0001
FLOOR = 2e-4
GAIN = 25.0
SPEEDS = [(a, b, c) for a in (-1, 0, 1) for b in (-1, 0, 1) for c in (-1, 0, 1)]
WTABLE = (8.0 / 27.0, 2.0 / 27.0, 1.0 / 54.0, 1.0 / 216.0)
CLASS = [a * a + b * b + c * c for a, b, c in SPEEDS]
PAIRS = list(range(14, 27))
PW = [WTABLE[CLASS[i]] for i in PAIRS]
W0 = WTABLE[0]
DIRS = [(1, 0), (-1, 0), (0, 1), (0, -1), (1, 1), (1, -1), (-1, 1), (-1, -1)]
TILE = 8


def moving(dx, dy, sign):
    return [
        i
        for i, (a, b, c) in enumerate(SPEEDS)
        if (dx == 0 or a == sign * dx) and (dy == 0 or b == sign * dy)
    ]


def quad(xx, yy, zz, xy, xz, yz):
    xpy, xpz, ypz = xx + yy, xx + zz, yy + zz
    tot = xpy + zz
    s1, s2 = tot + xy, tot - xy
    a, b = xz + yz, xz - yz
    return [
        zz, ypz - yz, yy, ypz + yz,
        s2 - b, xpy - xy, s2 + b,
        xpz - xz, xx, xpz + xz,
        s1 - a, xpy + xy, s1 + a,
    ]


def linear(x, y, z):
    xmy, xpy = x - y, x + y
    return [z, y - z, y, y + z, xmy - z, xmy, xmy + z, x - z, x, x + z, xpy - z, xpy, xpy + z]


def even_moments(e):
    e14, e15, e16, e17, e18, e19, e20, e21, e22, e23, e24, e25, e26 = e
    a, b, n, c = e18 + e20, e24 + e26, e21 + e23, e15 + e17
    m, p, cy = a + e19, b + e25, c + e16
    mp = m + p
    xx = mp + (n + e22)
    yy = cy + mp
    zz = (e14 + c) + (a + b) + n
    d18, d24, d21, d15 = e20 - e18, e26 - e24, e23 - e21, e17 - e15
    total = xx + cy + e14
    return total, xx, yy, zz, p - m, d18 + d24 + d21, d15 + d24 - d18


def odd_moments(o):
    o14, o15, o16, o17, o18, o19, o20, o21, o22, o23, o24, o25, o26 = o
    m, p = o18 + o19 + o20, o24 + o25 + o26
    x = m + p + (o21 + o22 + o23)
    y = (o15 + o16 + o17) + p - m
    z = o14 + (o17 - o15) + (o20 - o18) + (o26 - o24) + (o23 - o21)
    return x, y, z


def by_class(values):
    sums = {}
    for i, v in zip(PAIRS, values):
        sums[CLASS[i]] = v if CLASS[i] not in sums else sums[CLASS[i]] + v
    return sums


def split(f):
    even = [f[i] + f[26 - i] for i in PAIRS]
    odd = [f[i] - f[26 - i] for i in PAIRS]
    return even, odd, f[13]


def prepare(even, odd, f0, resist):
    total, xx, yy, zz, xy, xz, yz = even_moments(even)
    rho = total + f0
    j = odd_moments(odd)
    force = [rho * BODY_FORCE - resist * j[0], -resist * j[1], -resist * j[2]]
    inv = 1.0 / rho
    v = [j[a] + 0.5 * force[a] for a in range(3)]
    u = [v[a] * inv for a in range(3)]
    uv = [u[0] * v[0], u[1] * v[1], u[2] * v[2], u[0] * v[1], u[0] * v[2], u[1] * v[2]]
    third = rho * (1.0 / 3.0)
    pi = [xx - third, yy - third, zz - third, xy, xz, yz]
    stress = [pi[k] - uv[k] for k in range(6)]
    trace = stress[0] + stress[1] + stress[2]
    base = rho - 1.5 * (uv[0] + uv[1] + uv[2])
    q0 = trace * (-1.0 / 3.0)
    q = quad(
        stress[0] + q0, stress[1] + q0, stress[2] + q0, 2.0 * stress[3], 2.0 * stress[4], 2.0 * stress[5]
    )
    q = [val + (1 - CLASS[i]) * q0 if CLASS[i] != 1 else val for i, val in zip(PAIRS, q)]
    low = base - 1.5 * trace
    t2 = quad(*[4.5 * pi[k] for k in range(3)], *[9.0 * pi[k] for k in range(3, 6)])
    cv = linear(*v)
    he = [even[n] - (2.0 * PW[n]) * (low + t2[n]) for n in range(13)]
    ho = [odd[n] - (6.0 * PW[n]) * cv[n] for n in range(13)]
    h0 = f0 - W0 * low
    qq = by_class([val * val for val in q])
    ss = 40.5 * (WTABLE[1] * qq[1] + WTABLE[2] * qq[2] + WTABLE[3] * qq[3]) + (20.25 * W0) * (q0 * q0)
    sh = q0 * h0
    for n in range(13):
        sh = sh + q[n] * he[n]
    sh = 4.5 * sh
    hs = by_class([he[n] * he[n] + ho[n] * ho[n] for n in range(13)])
    hh = (
        (0.5 / WTABLE[1]) * hs[1] + (0.5 / WTABLE[2]) * hs[2] + (0.5 / WTABLE[3]) * hs[3]
        + (1.0 / W0) * (h0 * h0)
    )
    size = ss + hh
    inv_size = 1.0 / jnp.maximum(size, FLOOR)
    ratio = sh * inv_size
    gamma = 1.0 / BETA - KAPPA * ratio
    return dict(
        even=even, odd=odd, f0=f0, resist=resist, rho=rho, j=j, force=force, inv=inv, v=v, u=u, uv=uv,
        stress=stress, trace=trace, base=base, q=q, q0=q0, he=he, ho=ho, h0=h0, size=size,
        inv_size=inv_size, ratio=ratio, gamma=gamma,
    )


def relax(s):
    bg = BETA * s["gamma"]
    keep = 1.0 - bg
    kap = bg - 2.0 * BETA
    u, v, force = s["u"], s["v"], s["force"]
    uf = u[0] * force[0] + u[1] * force[1] + u[2] * force[2]
    const = bg * s["base"] - 1.5 * kap * s["trace"] - (3.0 * (1.0 - BETA)) * uf
    src = 9.0 * (1.0 - BETA)
    b45, k45, b9, k9 = 4.5 * bg, 4.5 * kap, 9.0 * bg, 9.0 * kap
    uv, st = s["uv"], s["stress"]
    t = [b45 * uv[a] + k45 * st[a] + src * (u[a] * force[a]) for a in range(3)]
    for n, (a, b) in enumerate(((0, 1), (0, 2), (1, 2))):
        t.append(b9 * uv[3 + n] + k9 * st[3 + n] + src * (u[a] * force[b] + u[b] * force[a]))
    tq = quad(*t)
    ck = linear(*[bg * v[a] + (1.0 - BETA) * force[a] for a in range(3)])
    even = [keep * s["even"][n] + (2.0 * PW[n]) * (const + tq[n]) for n in range(13)]
    odd = [keep * s["odd"][n] + (6.0 * PW[n]) * ck[n] for n in range(13)]
    return even, odd, keep * s["f0"] + W0 * const


def pull(s, me, mo, m0):
    bg = BETA * s["gamma"]
    keep = 1.0 - bg
    kap = bg - 2.0 * BETA
    u, v, force, uv, st = s["u"], s["v"], s["force"], s["uv"], s["stress"]
    q, q0, he, ho, h0 = s["q"], s["q0"], s["he"], s["ho"], s["h0"]
    off = ((0, 1), (0, 2), (1, 2))

    keep_bar = m0 * s["f0"]
    for n in range(13):
        keep_bar = keep_bar + (me[n] * s["even"][n] + mo[n] * s["odd"][n])
    mom = even_moments([(2.0 * PW[n]) * me[n] for n in range(13)])
    const_bar = mom[0] + W0 * m0
    tb = mom[1:]
    kb = odd_moments([(6.0 * PW[n]) * mo[n] for n in range(13)])
    bg_bar = (
        const_bar * s["base"]
        + 4.5 * (tb[0] * uv[0] + tb[1] * uv[1] + tb[2] * uv[2])
        + 9.0 * (tb[3] * uv[3] + tb[4] * uv[4] + tb[5] * uv[5])
        + (kb[0] * v[0] + kb[1] * v[1] + kb[2] * v[2])
    )
    kap_bar = (
        -1.5 * s["trace"] * const_bar
        + 4.5 * (tb[0] * st[0] + tb[1] * st[1] + tb[2] * st[2])
        + 9.0 * (tb[3] * st[3] + tb[4] * st[4] + tb[5] * st[5])
    )
    gamma_bar = BETA * (bg_bar + kap_bar - keep_bar)
    base_bar = bg * const_bar
    uf_bar = (-3.0 * (1.0 - BETA)) * const_bar

    scaled = KAPPA * gamma_bar * s["inv_size"]
    sh_bar = -4.5 * scaled
    size_bar = jnp.where(s["size"] > FLOOR, scaled * s["ratio"], 0.0)
    by_w = {k: size_bar * (1.0 / WTABLE[k]) for k in (1, 2, 3)}
    heb = [by_w[CLASS[i]] * he[n] + sh_bar * q[n] for n, i in enumerate(PAIRS)]
    hob = [by_w[CLASS[i]] * ho[n] for n, i in enumerate(PAIRS)]
    h0b = (size_bar * (2.0 / W0)) * h0 + sh_bar * q0
    by_q = {k: size_bar * (81.0 * WTABLE[k]) for k in (1, 2, 3)}
    qb = [sh_bar * he[n] + by_q[CLASS[i]] * q[n] for n, i in enumerate(PAIRS)]
    q0b = sh_bar * h0 + (size_bar * (40.5 * W0)) * q0

    hm = even_moments([(2.0 * PW[n]) * heb[n] for n in range(13)])
    low_bar = -(hm[0] + W0 * h0b)
    t2 = [-x for x in hm[1:]]
    hv = odd_moments([(6.0 * PW[n]) * hob[n] for n in range(13)])
    qm = even_moments(qb)
    q_all = (qm[0] + q0b) * (1.0 / 3.0)
    base_bar = base_bar + low_bar
    k45, k9 = 4.5 * kap, 9.0 * kap
    common = -1.5 * (kap * const_bar + low_bar) - q_all
    pb = [k45 * tb[a] + 4.5 * t2[a] + qm[1 + a] + common for a in range(3)]
    pb += [k9 * tb[a] + 9.0 * t2[a] + 2.0 * qm[1 + a] for a in range(3, 6)]

    that = [9.0 * tb[k] for k in range(6)]
    qhat = [bg * that[k] + 9.0 * t2[k] - (2.0 if k < 3 else 1.0) * pb[k] for k in range(6)]

    def apply(m, x):
        return [
            m[0] * x[0] + m[3] * x[1] + m[4] * x[2],
            m[3] * x[0] + m[1] * x[1] + m[5] * x[2],
            m[4] * x[0] + m[5] * x[1] + m[2] * x[2],
        ]

    qu = apply(qhat, u)
    tf = apply(that, force)
    tu = apply(that, u)
    rest = [((1.0 - BETA) * tf[a] + uf_bar * force[a]) * s["inv"] for a in range(3)]
    usq = u[0] * u[0] + u[1] * u[1] + u[2] * u[2]
    rho_bar = (
        base_bar * (1.0 + 1.5 * usq)
        - (pb[0] + pb[1] + pb[2]) * (1.0 / 3.0)
        - 0.5 * (u[0] * qu[0] + u[1] * qu[1] + u[2] * qu[2])
        - (u[0] * rest[0] + u[1] * rest[1] + u[2] * rest[2])
    )
    b3 = 3.0 * base_bar
    vb = [bg * kb[a] - hv[a] + qu[a] - b3 * u[a] + rest[a] for a in range(3)]
    fb = [(1.0 - BETA) * (kb[a] + tu[a]) + uf_bar * u[a] + 0.5 * vb[a] for a in range(3)]
    rho_bar = rho_bar + BODY_FORCE * fb[0]
    jb = [vb[a] - s["resist"] * fb[a] for a in range(3)]
    resist_bar = -(s["j"][0] * fb[0] + s["j"][1] * fb[1] + s["j"][2] * fb[2])
    pq = quad(*pb)
    jl = linear(*jb)
    eb = [keep * me[n] + heb[n] + rho_bar + pq[n] for n in range(13)]
    ob = [keep * mo[n] + hob[n] + jl[n] for n in range(13)]
    return eb, ob, keep * m0 + h0b + rho_bar, resist_bar


def kernel(
    nx, ny, cp_hbm, la_ref, res_hbm, mask_hbm, out_ref, sens_ref, cp_ref, res_ref, mask_ref,
    g, st, aux, fl, acc, ys, yr, cs, cr, ys0, yr0, cs0, cr0, sums, aux_sens,
    send, recv, send0, recv0, sum_send, sum_recv, in_sem,
):
    ext_x, ext_y, lanes = res_ref.shape
    tiles = ext_y // TILE
    chunks = ext_x * tiles
    top, end = TILE, TILE + ext_y
    px, py = lax.axis_index("gx"), lax.axis_index("gy")

    def device(dx, dy):
        return (lax.rem(px + (dx + nx), nx), lax.rem(py + (dy + ny), ny))

    partners = set((dx % nx, dy % ny) for dx, dy in DIRS)
    partners |= set((0, d) for d in range(1, ny)) | set((d, 0) for d in range(1, nx))
    partners = sorted(partners)
    barrier = pltpu.get_barrier_semaphore()
    for dx, dy in partners:
        pl.semaphore_signal(barrier, inc=1, device_id=device(dx, dy), device_id_type=MESH)

    la_copy = pltpu.make_async_copy(
        la_ref, g.at[2, :, pl.ds(1, ext_x), pl.ds(top, ext_y), :], in_sem.at[3]
    )
    loads = [
        pltpu.make_async_copy(cp_hbm, cp_ref, in_sem.at[0]),
        pltpu.make_async_copy(res_hbm, res_ref, in_sem.at[1]),
        pltpu.make_async_copy(mask_hbm, mask_ref, in_sem.at[2]),
    ]
    for copy in loads:
        copy.start()
    la_copy.start()
    for copy in loads:
        copy.wait()
    fl[pl.ds(1, ext_x), pl.ds(top, ext_y), :] = 1.0 - mask_ref[...].astype(jnp.float32)

    def exchange(par, sign, first=False):
        ss, rs = (send0, recv0) if first else (send.at[par % 2], recv.at[par % 2])
        ysr, yrr = (ys0, yr0) if first else (ys.at[par % 2], yr.at[par % 2])
        csr, crr = (cs0, cr0) if first else (cs.at[par % 2], cr.at[par % 2])
        copies = []
        for d, (dx, dy) in enumerate(DIRS):
            if dy == 0:
                pops = moving(dx, 0, sign)
                lo = pops[0]
                near, far = (ext_x, 0) if dx > 0 else (1, ext_x + 1)
                rows = pl.ds(top, ext_y)
                src = g.at[par, pl.ds(lo, 9), near, rows, :]
                dst = g.at[par, pl.ds(lo, 9), far, rows, :]
            elif dx == 0:
                src, dst = ysr.at[d - 2], yrr.at[d - 2]
            else:
                src, dst = csr.at[d - 4], crr.at[d - 4]
            copies.append(
                pltpu.make_async_remote_copy(
                    src_ref=src, dst_ref=dst, send_sem=ss.at[d], recv_sem=rs.at[d],
                    device_id=device(dx, dy), device_id_type=MESH,
                )
            )
        if first:
            for d, (dx, dy) in enumerate(DIRS[:2]):
                near, far = (ext_x, 0) if dx > 0 else (1, ext_x + 1)
                rows = pl.ds(top, ext_y)
                copies.append(
                    pltpu.make_async_remote_copy(
                        src_ref=fl.at[near, rows, :], dst_ref=fl.at[far, rows, :],
                        send_sem=ss.at[8 + d], recv_sem=rs.at[8 + d],
                        device_id=device(dx, 0), device_id_type=MESH,
                    )
                )

        def pack_rows(unpack, which):
            for d in which:
                dx, dy = DIRS[d]
                pops = moving(dx, dy, sign)
                if unpack:
                    row = top - 1 if dy > 0 else end
                    planes = [0 if dx > 0 else ext_x + 1] if dx else range(1, ext_x + 1)
                else:
                    row = end - 1 if dy > 0 else top
                    planes = [ext_x if dx > 0 else 1] if dx else range(1, ext_x + 1)
                box = (yrr if unpack else ysr) if dx == 0 else (crr if unpack else csr)
                k = d - 2 if dx == 0 else d - 4
                n = 0
                for i in pops:
                    for x in planes:
                        if unpack:
                            g[par, i, x, pl.ds(row, 1), :] = box[k, pl.ds(n, 1), :]
                        else:
                            box[k, pl.ds(n, 1), :] = g[par, i, x, pl.ds(row, 1), :]
                        n += 1
                if first:
                    for x in planes:
                        if unpack:
                            fl[x, pl.ds(row, 1), :] = box[k, pl.ds(n, 1), :]
                        else:
                            box[k, pl.ds(n, 1), :] = fl[x, pl.ds(row, 1), :]
                        n += 1

        def start_outer():
            pack_rows(False, (4, 5, 6, 7))
            for copy in copies[4:8] + copies[:2] + copies[8:]:
                copy.start()

        def start_row(d):
            pack_rows(False, (d,))
            copies[d].start()

        def finish(which):
            done = copies[:2] + copies[4:] if which == 4 else [copies[which]]
            for copy in done:
                copy.wait_recv()
            for copy in done:
                copy.wait_send()
            pack_rows(True, (4, 5, 6, 7) if which == 4 else (which,))

        return start_outer, start_row, finish

    def sweep(body, flip, sends=None, waits=None):
        early, late = (2, 3) if flip else (3, 2)
        wide = ext_x - 2

        def step(c, carry):
            if waits is not None:
                @pl.when(c == 2 * (tiles - 1))
                def _():
                    waits(early)
            side = c < 2 * tiles
            k = c - 2 * tiles
            t = jnp.where(side, c // 2, k // wide)
            x = jnp.where(side, lax.rem(c, 2) * (ext_x - 1), 1 + lax.rem(k + 2 * wide * tiles, wide))
            if flip:
                t = tiles - 1 - t
            body(x, pl.multiple_of(t * TILE, TILE))
            if sends is not None:
                start_outer, start_row = sends

                @pl.when(c == 2 * tiles - 1)
                def _():
                    start_outer()

                @pl.when(c == 2 * tiles + wide - 1)
                def _():
                    start_row(early)
            return carry

        if waits is not None:
            waits(4)
            waits(late)
        lax.fori_loop(0, chunks, step, 0)
        if sends is not None:
            sends[1](late)

    def place(c):
        x, t = c // tiles, lax.rem(c, tiles)
        return x, pl.multiple_of(t * TILE, TILE)

    def rolled(value, shift):
        return pltpu.roll(value, shift % lanes, 1) if shift else value

    def gather(par, x, row, sign):
        return [
            rolled(g[par, i, x + (1 - sign * a), pl.ds(row + (top - sign * b), TILE), :], sign * c)
            for i, (a, b, c) in enumerate(SPEEDS)
        ]

    def fluid_at(x, row, i):
        a, b, c = SPEEDS[i]
        return rolled(fl[x + (1 + a), pl.ds(row + (top + b), TILE), :], -c)

    def collided(f, x, row):
        solid = mask_ref[x, pl.ds(row, TILE), :] == 1
        even, odd, f0 = split(f)
        ne, no, n0 = relax(prepare(even, odd, f0, res_ref[x, pl.ds(row, TILE), :]))
        ne = [jnp.where(solid, even[n], ne[n]) * 0.5 for n in range(13)]
        no = [jnp.where(solid, -odd[n], no[n]) * 0.5 for n in range(13)]
        return ne, no, jnp.where(solid, f0, n0)

    def store_pairs(write, even, odd, f0):
        for n, i in enumerate(PAIRS):
            write(i, even[n] + odd[n])
            write(26 - i, even[n] - odd[n])
        write(13, f0)

    def into(par, x, row):
        def write(i, value):
            g[par, i, x + 1, pl.ds(row + top, TILE), :] = value
        return write

    def first_step(x, row):
        f = [cp_ref[i, x, pl.ds(row, TILE), :] for i in range(27)]
        store_pairs(into(0, x, row), *collided(f, x, row))

    start_outer, start_row, finish = exchange(0, 1)
    sweep(first_step, 0)
    pl.semaphore_wait(barrier, len(partners))
    start_outer()
    start_row(3)
    start_row(2)
    la_copy.wait()
    outer_la, row_la, finish_la = exchange(2, -1, first=True)
    outer_la()
    row_la(3)
    row_la(2)
    for step in (1, 2):
        def forward_step(x, row, step=step):
            f = gather((step - 1) % 2, x, row, 1)
            for i in range(27):
                st[step - 1, i, x, pl.ds(row, TILE), :] = f[i]
            store_pairs(into(step % 2, x, row), *collided(f, x, row))

        start_outer, start_row, later = exchange(step % 2, 1)
        sweep(forward_step, step % 2, (start_outer, start_row), finish)
        finish = later
    for d in (4, 3, 2):
        finish_la(d)
    acc[0] = jnp.zeros((TILE, lanes), jnp.float32)

    def last_step(x, row):
        f = gather(0, x, row, 1)
        for i in range(27):
            st[2, i, x, pl.ds(row, TILE), :] = f[i]
        ne, no, n0 = collided(f, x, row)
        flux = acc[0]
        for n, i in enumerate(PAIRS):
            if SPEEDS[i][0]:
                flux = flux + (
                    (ne[n] + no[n]) * fluid_at(x, row, i) - (ne[n] - no[n]) * fluid_at(x, row, 26 - i)
                )
        acc[0] = flux

    sweep(last_step, 1, None, finish)

    def spread(slot, base, count, axis):
        copies = []
        for d in range(1, count):
            copies.append(
                pltpu.make_async_remote_copy(
                    src_ref=acc.at[slot], dst_ref=sums.at[base + d - 1],
                    send_sem=sum_send.at[base + d - 1], recv_sem=sum_recv.at[base + d - 1],
                    device_id=device(d, 0) if axis == 0 else device(0, d), device_id_type=MESH,
                )
            )
        return copies

    along_y, along_x = spread(0, 0, ny, 1), spread(1, ny - 1, nx, 0)
    for copy in along_y:
        copy.start()

    def write_back(write, me, mo, m0, eb, ob, b0, solid):
        eb = [jnp.where(solid, me[n], eb[n]) for n in range(13)]
        ob = [jnp.where(solid, -mo[n], ob[n]) for n in range(13)]
        store_pairs(write, eb, ob, jnp.where(solid, m0, b0))

    def halves(m):
        even, odd, m0 = split(m)
        return [0.5 * e for e in even], [0.5 * o for o in odd], m0

    def adjoint_first(c, carry):
        x, row = place(c)
        rows = pl.ds(row, TILE)
        solid = mask_ref[x, rows, :] == 1
        f = [st[2, i, x, rows, :] for i in range(27)]
        s = prepare(*split(f), res_ref[x, rows, :])
        me, mo, m0 = halves(gather(2, x, row, -1))
        eb, ob, b0, rb = pull(s, me, mo, m0)
        write_back(into(1, x, row), me, mo, m0, eb, ob, b0, solid)
        sens_ref[x, rows, :] = jnp.where(solid, 0.0, rb)
        zero = jnp.zeros((TILE, lanes), jnp.float32)
        me, mo = [zero] * 13, [zero] * 13
        for n, i in enumerate(PAIRS):
            if SPEEDS[i][0]:
                ahead, behind = fluid_at(x, row, i), fluid_at(x, row, 26 - i)
                me[n], mo[n] = (0.5 * GAIN) * (ahead - behind), (0.5 * GAIN) * (ahead + behind)
        eb, ob, b0, rb = pull(s, me, mo, zero)

        def write(i, value):
            aux[i, x, rows, :] = value

        write_back(write, me, mo, zero, eb, ob, b0, solid)
        aux_sens[x, rows, :] = jnp.where(solid, 0.0, rb)
        return carry

    half = chunks // 2
    lax.fori_loop(0, half, adjoint_first, 0)
    for copy in along_y:
        copy.wait()
    total = acc[0]
    for d in range(ny - 1):
        total = total + sums[d]
    acc[1] = total
    for copy in along_x:
        copy.start()
    lax.fori_loop(half, chunks, adjoint_first, 0)
    for copy in along_x:
        copy.wait()
    for d in range(ny - 1, ny + nx - 2):
        total = total + sums[d]
    nodes = ext_x * ext_y * lanes * nx * ny
    mean = jnp.broadcast_to(jnp.sum(total, keepdims=True) * (1.0 / nodes), (TILE, lanes))

    def combine(x, row):
        rows = pl.ds(row, TILE)
        at = pl.ds(row + top, TILE)
        for i in range(27):
            g[1, i, x + 1, at, :] = g[1, i, x + 1, at, :] + mean * aux[i, x, rows, :]
        sens_ref[x, rows, :] = sens_ref[x, rows, :] + mean * aux_sens[x, rows, :]

    start_outer, start_row, finish = exchange(1, -1)
    sweep(combine, 0, (start_outer, start_row))

    for step in (2, 1, 0):
        par = (step + 1) % 2

        def adjoint_step(x, row, step=step, par=par):
            rows = pl.ds(row, TILE)
            solid = mask_ref[x, rows, :] == 1
            if step:
                f = [st[step - 1, i, x, rows, :] for i in range(27)]
            else:
                f = [cp_ref[i, x, rows, :] for i in range(27)]
            s = prepare(*split(f), res_ref[x, rows, :])
            me, mo, m0 = halves(gather(par, x, row, -1))
            eb, ob, b0, rb = pull(s, me, mo, m0)

            def write(i, value):
                if step:
                    g[step % 2, i, x + 1, pl.ds(row + top, TILE), :] = value
                else:
                    out_ref[i, x, rows, :] = value

            write_back(write, me, mo, m0, eb, ob, b0, solid)
            sens_ref[x, rows, :] = sens_ref[x, rows, :] + jnp.where(solid, 0.0, rb)

        if step:
            start_outer, start_row, later = exchange(step % 2, -1)
            sweep(adjoint_step, (step + 1) % 2, (start_outer, start_row), finish)
            finish = later
        else:
            sweep(adjoint_step, 1, None, finish)


def solution(mesh):
    nx, ny = mesh.shape["gx"], mesh.shape["gy"]

    def shards(checkpoint, later_adjoint, resistance, solid_mask):
        ext_x, ext_y, lanes = resistance.shape
        f32 = jnp.float32
        rows_x = 9 * ext_x
        vmem = pl.BlockSpec(memory_space=pltpu.VMEM)
        padded = (ext_x + 2, ext_y + 2 * TILE, lanes)
        count = nx + ny - 2
        return pl.pallas_call(
            functools.partial(kernel, nx, ny),
            out_shape=(
                jax.ShapeDtypeStruct(checkpoint.shape, f32),
                jax.ShapeDtypeStruct(resistance.shape, f32),
            ),
            in_specs=[pl.BlockSpec(memory_space=pltpu.HBM)] * 4,
            out_specs=(vmem, vmem),
            scratch_shapes=[
                pltpu.VMEM(checkpoint.shape, f32),
                pltpu.VMEM(resistance.shape, f32),
                pltpu.VMEM(solid_mask.shape, jnp.int32),
                pltpu.VMEM((3, 27) + padded, f32),
                pltpu.VMEM((3, 27, ext_x, ext_y, lanes), f32),
                pltpu.VMEM((27, ext_x, ext_y, lanes), f32),
                pltpu.VMEM(padded, f32),
                pltpu.VMEM((2, TILE, lanes), f32),
                pltpu.VMEM((2, 2, rows_x, lanes), f32),
                pltpu.VMEM((2, 2, rows_x, lanes), f32),
                pltpu.VMEM((2, 4, 3, lanes), f32),
                pltpu.VMEM((2, 4, 3, lanes), f32),
                pltpu.VMEM((2, rows_x + ext_x, lanes), f32),
                pltpu.VMEM((2, rows_x + ext_x, lanes), f32),
                pltpu.VMEM((4, 4, lanes), f32),
                pltpu.VMEM((4, 4, lanes), f32),
                pltpu.VMEM((count, TILE, lanes), f32),
                pltpu.VMEM((ext_x, ext_y, lanes), f32),
                pltpu.SemaphoreType.DMA((2, 8)),
                pltpu.SemaphoreType.DMA((2, 8)),
                pltpu.SemaphoreType.DMA((10,)),
                pltpu.SemaphoreType.DMA((10,)),
                pltpu.SemaphoreType.DMA((count,)),
                pltpu.SemaphoreType.DMA((count,)),
                pltpu.SemaphoreType.DMA((4,)),
            ],
            compiler_params=pltpu.CompilerParams(
                collective_id=0, has_side_effects=True, vmem_limit_bytes=60 * 1024 * 1024
            ),
        )(checkpoint, later_adjoint, resistance, solid_mask)

    placed = (
        P(None, "gx", "gy", None),
        P(None, "gx", "gy", None),
        P("gx", "gy", None),
        P("gx", "gy", None),
    )
    return jax.shard_map(
        shards,
        mesh=mesh,
        in_specs=placed,
        out_specs=(P(None, "gx", "gy", None), P("gx", "gy", None)),
        check_vma=False,
    )
```
